512 devices in a mesh: gz: 64 (over y, x, core), gy: 8 (over z).
Axes of the slice: x: 4, y: 8, z: 8, core: 2. Of those that a mesh axis runs over, the one named last changes fastest.
Arguments:
- fields: float32 [2, 512, 256, 512], P(None, 'gz', 'gy'), may hold values from 0 to 1
- classes: int32 [512, 256, 512], P('gz', 'gy'), may hold values from 0 to 7
- diff_table: float32 [2, 8], replicated, may hold values from 0.03 to 0.15
- transfer: float32 [4, 16], replicated, may hold values from 0.25 to 2
- bin_table: int32 [8], replicated, may hold values from 0 to 15
Outputs:
- species_out: float32 [2, 512, 256, 512], P(None, 'gz', 'gy')
- image: float32 [4, 131072], P(None, ('gy', 'gz'))
The draws below stay inside these ranges and needn't reach their ends.
All inputs are finite; a program needn't handle non-finite values.
Results may differ from the reference program's by a relative error of at most 0.0003.
Values sent between devices are 32-bit elements; how exact they have to be, the bound alone decides.
A program may use at most 64 MiB of HBM per device.

```python
import math
import jax
import jax.numpy as jnp
from jax import lax

NX = 512
NCLASS = 8
NBIN = 16
STEPS = 2
NZ = 512
NY = 256


def with_ends(drawn, own_key, smallest, top_value):
    extent = drawn.shape
    place = [jax.random.randint(jax.random.fold_in(own_key, axis), (), 0, extent[axis]) for axis in range(len(extent))]
    drawn = drawn.at[tuple(place)].set(smallest)
    longest = extent.index(max(extent))
    place[longest] = (place[longest] + 1) % extent[longest]
    return drawn.at[tuple(place)].set(top_value)


def block_scale(stream_key, dims, split, smallest, top_value):
    loudness, own = 1.0, jax.random.fold_in(stream_key, 6)
    for axis_at, blocks in split:
        heights = jnp.exp(jax.random.uniform(jax.random.fold_in(own, axis_at), (blocks,), jnp.float32, smallest / len(split), top_value / len(split)))
        loudness = loudness * jnp.repeat(heights, dims[axis_at] // blocks).reshape([-1 if axis == axis_at else 1 for axis in range(len(dims))])
    return loudness


def setup_inputs(seed: int = 0) -> dict:
    key_of = jax.random.split(jax.random.key(seed), 6)
    return {
        "fields": jnp.clip(1.0 * jax.random.uniform(key_of[0], (2, NZ, NY, NX), jnp.float32) ** block_scale(key_of[0], (2, NZ, NY, NX), ((1, 64), (2, 8)), -0.2, 0.2), 0.0, 1.0),
        "classes": with_ends(jax.random.randint(key_of[1], (NZ, NY, NX), 0, NCLASS), jax.random.fold_in(key_of[1], 1), 0, NCLASS - 1).astype(jnp.int32),
        "diff_table": jnp.clip(jnp.exp(jax.random.uniform(key_of[2], (2, NCLASS), jnp.float32, math.log(0.03), math.log(0.15))), 0.03, 0.15),
        "transfer": jnp.clip(jax.random.uniform(key_of[3], (4, NBIN), jnp.float32, 0.25, 2.0), 0.25, 2.0),
        "bin_table": with_ends(jax.random.randint(key_of[4], (NCLASS,), 0, NBIN), jax.random.fold_in(key_of[4], 1), 0, NBIN - 1).astype(jnp.int32),
    }


FEED_RATE = 0.04
KILL_RATE = 0.06


def per_class(classes, class_table):
    result = jnp.zeros((class_table.shape[0],) + classes.shape, jnp.float32)
    for material in range(class_table.shape[1]):
        column = class_table[:, material].reshape((-1,) + (1,) * classes.ndim)
        result = jnp.where((classes == material)[None], column, result)
    return result


def advance(padded, centre, cell_rates):
    widened = jnp.pad(padded, ((0, 0), (0, 0), (0, 0), (1, 1)))
    neighbours = widened[:, 2:, 1:-1, 1:-1] + widened[:, :-2, 1:-1, 1:-1]
    neighbours = neighbours + widened[:, 1:-1, 2:, 1:-1] + widened[:, 1:-1, :-2, 1:-1]
    neighbours = neighbours + widened[:, 1:-1, 1:-1, 2:] + widened[:, 1:-1, 1:-1, :-2]
    spread = cell_rates * (neighbours - 6.0 * centre)
    activator = centre[0]
    inhibitor = centre[1]
    growth = activator * inhibitor * inhibitor
    new_first = activator + spread[0] - growth + FEED_RATE * (1.0 - activator)
    new_second = inhibitor + spread[1] + growth - (FEED_RATE + KILL_RATE) * inhibitor
    return jnp.stack([new_first, new_second])


def render(fields, classes, colours, depth_step):
    def absorb(state_pair, planes):
        colour, transmit = state_pair
        activator, inhibitor, material = planes
        lookup = per_class(material, colours)
        extinction = lookup[3] * (0.25 + inhibitor * inhibitor)
        opacity = 1.0 - jnp.exp(-extinction * depth_step)
        colour = colour + (transmit * opacity * activator)[None] * lookup[:3]
        transmit = transmit * (1.0 - opacity)
        return (colour, transmit), None

    plane_shape = classes.shape[1:]
    initial = (jnp.zeros((3,) + plane_shape, jnp.float32), jnp.ones(plane_shape, jnp.float32))
    final_pair, unused = lax.scan(absorb, initial, (fields[0], fields[1], classes))
    return final_pair


def reference(fields, classes, diff_table, transfer, bin_table):
    cell_rates = per_class(classes, diff_table)
    for repeat in range(STEPS):
        padded = jnp.pad(fields, ((0, 0), (1, 1), (1, 1), (0, 0)))
        fields = advance(padded, fields, cell_rates)
    colours = transfer[:, bin_table]
    colour, transmit = render(fields, classes, colours, 2.0 / NZ)
    image = jnp.concatenate([colour.reshape(3, NY * NX), (1.0 - transmit).reshape(1, NY * NX)], 0)
    return fields, image
```

```python
import functools

import jax
import jax.numpy as jnp
from jax import lax
from jax.experimental import pallas as pl
from jax.experimental.pallas import tpu as pltpu
from jax.sharding import Mesh
from jax.sharding import PartitionSpec as P

MESH = pl.DeviceIdType.MESH
NAMES = ("py", "px", "pc", "pz")
GZ = ("py", "px", "pc")
FEED_RATE = 0.04
KILL_RATE = 0.06
NCLASS = 8
DEPTH = 8
COLS = 512
HALF = 256
BLOCK = 8


def kernel(
    sizes, depth_step,
    fields, classes, diff_table, transfer, bin_table,
    species, image,
    pad0, pad1, final, cls, rates, look, mid, part,
    edge0, edge0_in, edge1, edge1_in,
    send_a, recv_a, send_b, recv_b,
    diff_s, trans_s, bin_s,
    load_sem, table_sem, out_sem, own_sem,
    z_send, z_recv, y_send, y_recv, a_send, a_recv, b_send, b_recv,
):
    ny, nx, nc, nz = sizes
    py, px, pc, pz = (lax.axis_index(name) for name in NAMES)
    slabs = ny * nx * nc
    groups = (ny * nx) // BLOCK
    slab = (py * nx + px) * nc + pc

    def slab_device(g):
        return (lax.div(g, nx * nc), lax.rem(lax.div(g, nc), nx), lax.rem(g, nc), pz)

    above = slab_device(lax.rem(slab + 1, slabs))
    below = slab_device(lax.rem(slab + slabs - 1, slabs))
    north = (py, px, pc, lax.rem(pz + nz - 1, nz))
    south = (py, px, pc, lax.rem(pz + 1, nz))
    team = nx * nc
    me_a = px * nc + pc

    def mate_a(j):
        i = lax.rem(me_a + j, team)
        return i, (py, lax.div(i, nc), lax.rem(i, nc), pz)

    def mate_b(j):
        i = lax.rem(py + j, ny)
        return i, (i, px, pc, pz)

    load_fields = pltpu.make_async_copy(fields, pad0.at[:, pl.ds(1, DEPTH)], load_sem.at[0])
    load_classes = pltpu.make_async_copy(classes, cls, load_sem.at[1])
    load_fields.start()
    load_classes.start()
    tables = [
        pltpu.make_async_copy(src, dst, table_sem.at[i])
        for i, (src, dst) in enumerate(((diff_table, diff_s), (transfer, trans_s), (bin_table, bin_s)))
    ]
    for copy in tables:
        copy.start()
    barrier = pltpu.get_barrier_semaphore()
    partners = [above, below, north, south]
    partners += [mate_a(j)[1] for j in range(1, team)] + [mate_b(j)[1] for j in range(1, ny)]
    for device in partners:
        pl.semaphore_signal(barrier, inc=1, device_id=device, device_id_type=MESH)
    pl.semaphore_wait(barrier, len(partners))

    def depth_copies(step, source, first, last, target):
        made = []
        for k in range(groups):
            rows = pl.ds(BLOCK * k, BLOCK)
            for side, device, layer, place in ((0, above, last, 0), (1, below, first, DEPTH + 1)):
                made.append(
                    pltpu.make_async_remote_copy(
                        src_ref=source.at[:, layer, rows],
                        dst_ref=target.at[:, place, rows],
                        send_sem=z_send.at[step, side, k],
                        recv_sem=z_recv.at[step, side, k],
                        device_id=device,
                        device_id_type=MESH,
                    )
                )
        return made

    depth0 = depth_copies(0, fields, 0, DEPTH - 1, pad0)
    for copy in depth0:
        copy.start()
    load_fields.wait()

    def row_copies(step, part_at, source, target, layers):
        return [
            pltpu.make_async_remote_copy(
                src_ref=source.at[side, :, layers],
                dst_ref=target.at[side, :, layers],
                send_sem=y_send.at[step, part_at, side],
                recv_sem=y_recv.at[step, part_at, side],
                device_id=device,
                device_id_type=MESH,
            )
            for side, device in ((0, south), (1, north))
        ]

    def pack_rows(source, target, layers):
        for s in range(2):
            for z in layers:
                target[0, s, z] = source[s, z + 1, BLOCK * groups - 1 : BLOCK * groups, :]
                target[1, s, z] = source[s, z + 1, 0:1, :]

    pack_rows(pad0, edge0, range(DEPTH))
    rows0 = row_copies(0, 0, edge0, edge0_in, pl.ds(0, DEPTH))
    for copy in rows0:
        copy.start()

    for copy in tables:
        copy.wait()
    load_classes.wait()

    def class_bits(z, k):
        c = cls[z, BLOCK * k : BLOCK * k + BLOCK, :]
        return [(c & bit) != 0 for bit in (1, 2, 4)]

    def pick(bits, values):
        for bit in bits:
            values = [jnp.where(bit, high, low) for low, high in zip(values[::2], values[1::2])]
        return values[0]

    def look_up(target, values):
        splat = [[jnp.full((BLOCK, COLS), x, jnp.float32) for x in v] for v in values]

        def body(z, carry):
            for k in range(groups):
                bits = class_bits(z, k)
                for s, v in enumerate(splat):
                    target[s, z, BLOCK * k : BLOCK * k + BLOCK, :] = pick(bits, v)
            return carry

        lax.fori_loop(0, DEPTH, body, 0)

    look_up(rates, [[diff_s[s, m] for m in range(NCLASS)] for s in range(2)])

    sub = lax.broadcasted_iota(jnp.int32, (BLOCK, COLS), 0)
    col = lax.broadcasted_iota(jnp.int32, (BLOCK, COLS), 1)
    top, bottom = sub == 0, sub == BLOCK - 1
    left, right = col == 0, col == COLS - 1

    def around(source, edges, s, z, k):
        rows = slice(BLOCK * k, BLOCK * k + BLOCK)
        centre = source[s, z + 1, rows, :]
        if k == 0:
            before = edges[0, s, z]
        else:
            before = source[s, z + 1, BLOCK * k - 1 : BLOCK * k, :]
        if k == groups - 1:
            after = edges[1, s, z]
        else:
            after = source[s, z + 1, BLOCK * k + BLOCK : BLOCK * k + BLOCK + 1, :]
        total = source[s, z + 2, rows, :] + source[s, z, rows, :]
        total = total + jnp.where(bottom, after, pltpu.roll(centre, BLOCK - 1, 0))
        total = total + jnp.where(top, before, pltpu.roll(centre, 1, 0))
        total = total + jnp.where(right, 0.0, pltpu.roll(centre, COLS - 1, 1))
        total = total + jnp.where(left, 0.0, pltpu.roll(centre, 1, 1))
        return centre, total - 6.0 * centre

    def advance(source, edges, z, k):
        rows = slice(BLOCK * k, BLOCK * k + BLOCK)
        u, lap_u = around(source, edges, 0, z, k)
        v, lap_v = around(source, edges, 1, z, k)
        growth = u * v * v
        new_u = u + rates[0, z, rows, :] * lap_u - growth + FEED_RATE * (1.0 - u)
        new_v = v + rates[1, z, rows, :] * lap_v + growth - (FEED_RATE + KILL_RATE) * v
        return new_u, new_v

    def first_update(z, k):
        new_u, new_v = advance(pad0, edge0_in, z, k)
        rows = slice(BLOCK * k, BLOCK * k + BLOCK)
        pad1[0, z + 1, rows, :] = new_u
        pad1[1, z + 1, rows, :] = new_v

    def clear_rows(target, layers):
        @pl.when(pz == 0)
        def _():
            for s in range(2):
                for z in layers:
                    target[0, s, z] = jnp.zeros((1, COLS), jnp.float32)

        @pl.when(pz == nz - 1)
        def _():
            for s in range(2):
                for z in layers:
                    target[1, s, z] = jnp.zeros((1, COLS), jnp.float32)

    def clear_depth(target, side, k):
        rows = slice(BLOCK * k, BLOCK * k + BLOCK)

        @pl.when(slab == (0 if side == 0 else slabs - 1))
        def _():
            for s in range(2):
                target[s, 0 if side == 0 else DEPTH + 1, rows, :] = jnp.zeros((BLOCK, COLS), jnp.float32)

    for copy in rows0:
        copy.wait_recv()
    clear_rows(edge0_in, range(DEPTH))

    def interior1(z, carry):
        for k in range(groups):
            first_update(z, k)
        return carry

    lax.fori_loop(1, DEPTH - 1, interior1, 0)
    pack_rows(pad1, edge1, range(1, DEPTH - 1))
    rows1 = row_copies(1, 0, edge1, edge1_in, pl.ds(1, DEPTH - 2))
    for copy in rows1:
        copy.start()

    depth1 = depth_copies(1, pad1, 1, DEPTH, pad1)
    for k in range(groups):
        for side in range(2):
            depth0[2 * k + side].wait_recv()
            clear_depth(pad0, side, k)
            first_update(0 if side == 0 else DEPTH - 1, k)
            depth1[2 * k + 1 - side].start()
    pack_rows(pad1, edge1, (0, DEPTH - 1))
    rows2 = row_copies(1, 1, edge1, edge1_in, pl.ds(0, 1)) + row_copies(1, 2, edge1, edge1_in, pl.ds(DEPTH - 1, 1))
    for copy in rows2:
        copy.start()

    bins = [bin_s[m] for m in range(NCLASS)]
    look_up(look, [[trans_s[c, b] for b in bins] for c in range(4)])

    def second_update(z, k):
        new_u, new_v = advance(pad1, edge1_in, z, k)
        rows = slice(BLOCK * k, BLOCK * k + BLOCK)
        final[0, z, rows, :] = new_u
        final[1, z, rows, :] = new_v
        passed = jnp.exp(look[3, z, rows, :] * (0.25 + new_v * new_v) * (-depth_step))
        return new_u, passed

    for copy in rows1:
        copy.wait_recv()
    clear_rows(edge1_in, range(1, DEPTH - 1))
    for k in range(groups):
        rows = slice(BLOCK * k, BLOCK * k + BLOCK)
        mid[3, rows, :] = jnp.ones((BLOCK, COLS), jnp.float32)
        for c in range(3):
            mid[c, rows, :] = jnp.zeros((BLOCK, COLS), jnp.float32)

    def interior2(z, carry):
        for k in range(groups):
            rows = slice(BLOCK * k, BLOCK * k + BLOCK)
            new_u, passed = second_update(z, k)
            transmit = mid[3, rows, :]
            weight = transmit * (1.0 - passed) * new_u
            for c in range(3):
                mid[c, rows, :] = mid[c, rows, :] + weight * look[c, z, rows, :]
            mid[3, rows, :] = transmit * passed
        return carry

    lax.fori_loop(1, DEPTH - 1, interior2, 0)

    for copy in rows2:
        copy.wait_recv()
    clear_rows(edge1_in, (0, DEPTH - 1))
    for k in range(groups):
        rows = slice(BLOCK * k, BLOCK * k + BLOCK)
        for side in range(2):
            depth1[2 * k + side].wait_recv()
            clear_depth(pad1, side, k)
        front_u, front_t = second_update(0, k)
        back_u, back_t = second_update(DEPTH - 1, k)
        front = (1.0 - front_t) * front_u
        transmit = mid[3, rows, :]
        back = transmit * (1.0 - back_t) * back_u
        values = [
            front * look[c, 0, rows, :] + front_t * (mid[c, rows, :] + back * look[c, DEPTH - 1, rows, :])
            for c in range(3)
        ]
        values.append(front_t * transmit * back_t)
        for c in range(4):
            for t in range(COLS // 128):
                part[c, t, rows, :] = values[c][:, 128 * t : 128 * t + 128]

    store = pltpu.make_async_copy(final, species, out_sem.at[0])
    store.start()

    tiles = COLS // 128 // nc
    for x in range(nx):
        for c in range(4):
            for t in range(COLS // 128):
                send_a[x * nc + t // tiles, c, :, 128 * (t % tiles) : 128 * (t % tiles) + 128] = part[
                    c, t, pl.ds(x, ny, stride=nx), :
                ]
    own = pltpu.make_async_copy(send_a.at[me_a], recv_a.at[me_a], own_sem.at[0])
    own.start()
    stage_a = []
    for j in range(1, team):
        i, device = mate_a(j)
        copy = pltpu.make_async_remote_copy(
            src_ref=send_a.at[i],
            dst_ref=recv_a.at[me_a],
            send_sem=a_send.at[j],
            recv_sem=a_recv.at[me_a],
            device_id=device,
            device_id_type=MESH,
        )
        copy.start()
        stage_a.append(copy)
    own.wait()
    for j in range(1, team):
        i, device = mate_a(j)
        pltpu.make_async_remote_copy(
            src_ref=send_a.at[i],
            dst_ref=recv_a.at[i],
            send_sem=a_send.at[j],
            recv_sem=a_recv.at[i],
            device_id=device,
            device_id_type=MESH,
        ).wait_recv()
    for t in range(HALF // 128):
        cols = slice(128 * t, 128 * t + 128)
        colour = [recv_a[0, c, :, cols] for c in range(3)]
        transmit = recv_a[0, 3, :, cols]
        for i in range(1, team):
            colour = [colour[c] + transmit * recv_a[i, c, :, cols] for c in range(3)]
            transmit = transmit * recv_a[i, 3, :, cols]
        for c, value in enumerate(colour + [transmit]):
            send_b[pl.ds(4 * t + c, ny, stride=8), :] = value

    own_b = pltpu.make_async_copy(send_b.at[pl.ds(pl.multiple_of(8 * py, 8), 8)], recv_b.at[py], own_sem.at[1])
    own_b.start()
    stage_b = []
    for j in range(1, ny):
        i, device = mate_b(j)
        copy = pltpu.make_async_remote_copy(
            src_ref=send_b.at[pl.ds(pl.multiple_of(8 * i, 8), 8)],
            dst_ref=recv_b.at[py],
            send_sem=b_send.at[j],
            recv_sem=b_recv.at[py],
            device_id=device,
            device_id_type=MESH,
        )
        copy.start()
        stage_b.append(copy)
    own_b.wait()
    for j in range(1, ny):
        i, device = mate_b(j)
        pltpu.make_async_remote_copy(
            src_ref=send_b.at[pl.ds(pl.multiple_of(8 * i, 8), 8)],
            dst_ref=recv_b.at[i],
            send_sem=b_send.at[j],
            recv_sem=b_recv.at[i],
            device_id=device,
            device_id_type=MESH,
        ).wait_recv()
    lower = lax.broadcasted_iota(jnp.int32, (8, 128), 0) < 4
    total = recv_b[0]
    transmit = None
    for i in range(ny):
        value = recv_b[i]
        light = jnp.where(lower, recv_b[i, 3:4, :], recv_b[i, 7:8, :])
        if i == 0:
            total, transmit = value, light
        else:
            total, transmit = total + transmit * value, transmit * light
    place = lax.broadcasted_iota(jnp.int32, (8, 128), 0)
    total = jnp.where((place == 3) | (place == 7), 1.0 - transmit, total)
    image[:, 0:128] = total[0:4, :]
    image[:, 128:256] = total[4:8, :]

    for copy in depth0 + rows0 + rows1 + depth1 + rows2 + stage_a + stage_b:
        copy.wait_send()
    store.wait()


def build(mesh, sizes):
    ny, nx, nc, nz = sizes
    rows = ny * nx
    groups = rows // BLOCK
    team = nx * nc
    f32 = jnp.float32

    def shards(fields, classes, diff_table, transfer, bin_table):
        depth_step = 2.0 / (DEPTH * ny * nx * nc)
        anywhere = pl.BlockSpec(memory_space=pl.ANY)
        return pl.pallas_call(
            functools.partial(kernel, sizes, depth_step),
            out_shape=(
                jax.ShapeDtypeStruct((2, DEPTH, rows, COLS), f32),
                jax.ShapeDtypeStruct((4, HALF), f32),
            ),
            in_specs=[anywhere] * 5,
            out_specs=(anywhere, pl.BlockSpec(memory_space=pltpu.VMEM)),
            scratch_shapes=[
                pltpu.VMEM((2, DEPTH + 2, rows, COLS), f32),
                pltpu.VMEM((2, DEPTH + 2, rows, COLS), f32),
                pltpu.VMEM((2, DEPTH, rows, COLS), f32),
                pltpu.VMEM((DEPTH, rows, COLS), jnp.int32),
                pltpu.VMEM((2, DEPTH, rows, COLS), f32),
                pltpu.VMEM((4, DEPTH, rows, COLS), f32),
                pltpu.VMEM((4, rows, COLS), f32),
                pltpu.VMEM((4, COLS // 128, rows, 128), f32),
                pltpu.VMEM((2, 2, DEPTH, 1, COLS), f32),
                pltpu.VMEM((2, 2, DEPTH, 1, COLS), f32),
                pltpu.VMEM((2, 2, DEPTH, 1, COLS), f32),
                pltpu.VMEM((2, 2, DEPTH, 1, COLS), f32),
                pltpu.VMEM((team, 4, ny, HALF), f32),
                pltpu.VMEM((team, 4, ny, HALF), f32),
                pltpu.VMEM((8 * ny, 128), f32),
                pltpu.VMEM((ny, 8, 128), f32),
                pltpu.SMEM((2, NCLASS), f32),
                pltpu.SMEM(transfer.shape, f32),
                pltpu.SMEM(bin_table.shape, jnp.int32),
                pltpu.SemaphoreType.DMA((2,)),
                pltpu.SemaphoreType.DMA((3,)),
                pltpu.SemaphoreType.DMA((1,)),
                pltpu.SemaphoreType.DMA((2,)),
                pltpu.SemaphoreType.DMA((2, 2, groups)),
                pltpu.SemaphoreType.DMA((2, 2, groups)),
                pltpu.SemaphoreType.DMA((2, 3, 2)),
                pltpu.SemaphoreType.DMA((2, 3, 2)),
                pltpu.SemaphoreType.DMA((team,)),
                pltpu.SemaphoreType.DMA((team,)),
                pltpu.SemaphoreType.DMA((ny,)),
                pltpu.SemaphoreType.DMA((ny,)),
            ],
            compiler_params=pltpu.CompilerParams(
                collective_id=0, has_side_effects=True
            ),
            name="gray_scott",
        )(fields, classes, diff_table, transfer, bin_table)

    finer = Mesh(mesh.devices.reshape(sizes), NAMES)
    return jax.shard_map(
        shards,
        mesh=finer,
        in_specs=(P(None, GZ, "pz", None), P(GZ, "pz", None), P(), P(), P()),
        out_specs=(P(None, GZ, "pz", None), P(None, ("pz",) + GZ)),
        check_vma=False,
    )


def solution(mesh):
    return build(mesh, (8, 4, 2, mesh.shape["gy"]))
```

```python
import functools

import jax
import jax.numpy as jnp
from jax import lax
from jax.experimental import pallas as pl
from jax.experimental.pallas import tpu as pltpu
from jax.sharding import Mesh
from jax.sharding import PartitionSpec as P

MESH = pl.DeviceIdType.MESH
NAMES = ("py", "px", "pc", "pz")
GZ = ("py", "px", "pc")
FEED_RATE = 0.04
KILL_RATE = 0.06
NCLASS = 8
DEPTH = 8
COLS = 512
LANES = 128
BLOCK = 8
F32 = jnp.float32


def span(k):
    return slice(BLOCK * k, BLOCK * k + BLOCK)


def kernel(
    sizes, depth_step,
    fields, classes, diff_table, transfer, bin_table,
    final, pixels,
    pad0, pad1, cls, rates, look, mid,
    edge0, edge0_in, edge1, edge1_in,
    halves, merged, gathered,
    diff_s, trans_s, bin_s,
    load_sem, class_sem, table_sem,
    z_send, z_recv, y_send, y_recv, c_send, c_recv, e_send, e_recv, relay,
):
    ny, nx, nc, nz = sizes
    py, px, pc, pz = (lax.axis_index(name) for name in NAMES)
    slabs = ny * nx * nc
    groups = (ny * nx) // BLOCK
    inner, outer = list(range(1, groups - 1)), [0, groups - 1]
    slab = (py * nx + px) * nc + pc
    chip = py * nx + px

    def slab_device(g):
        return (lax.div(g, nx * nc), lax.rem(lax.div(g, nc), nx), lax.rem(g, nc), pz)

    above = slab_device(lax.rem(slab + 1, slabs))
    below = slab_device(lax.rem(slab + slabs - 1, slabs))
    north = (py, px, pc, lax.rem(pz + nz - 1, nz))
    south = (py, px, pc, lax.rem(pz + 1, nz))
    mate = (py, px, 1 - pc, pz)
    has_above, has_below = slab < slabs - 1, slab > 0
    has_north, has_south = pz > 0, pz < nz - 1

    def shifted(dy, dx):
        return (lax.rem(py + dy, ny), lax.rem(px + dx, nx), pc, pz)

    loads = {
        k: pltpu.make_async_copy(
            fields.at[:, :, pl.ds(BLOCK * k, BLOCK)],
            pad0.at[:, pl.ds(1, DEPTH), pl.ds(BLOCK * k, BLOCK)],
            load_sem.at[k],
        )
        for k in outer + inner
    }
    for copy in loads.values():
        copy.start()
    tables = [
        pltpu.make_async_copy(src, dst, table_sem.at[i])
        for i, (src, dst) in enumerate(((diff_table, diff_s), (transfer, trans_s), (bin_table, bin_s)))
    ]
    for copy in tables:
        copy.start()
    load_classes = pltpu.make_async_copy(classes, cls, class_sem.at[0])
    load_classes.start()

    barrier = pltpu.get_barrier_semaphore()

    def greet(device):
        pl.semaphore_signal(barrier, inc=1, device_id=device, device_id_type=MESH)

    ring_y = (shifted(1, 0), shifted(ny - 1, 0))
    ring_x = (shifted(0, 1), shifted(0, nx - 1))
    partners = (mate,) + ring_x + ring_y
    others = ((has_above, above), (has_below, below), (has_north, north), (has_south, south))
    count = len(partners)
    for exists, device in others:
        pl.when(exists)(functools.partial(greet, device))
        count = count + jnp.where(exists, 1, 0)
    for device in partners:
        greet(device)
    pl.semaphore_wait(barrier, count)

    def pass_on(r, ring):
        for way in range(2):
            pl.semaphore_signal(relay.at[r, way], inc=1, device_id=ring[way], device_id_type=MESH)

    def heard(r):
        for way in range(2):
            pl.semaphore_wait(relay.at[r, way], 1)

    sends = {"up": has_above, "down": has_below, "south": has_south, "north": has_north}
    arrives = {"up": has_below, "down": has_above, "south": has_north, "north": has_south}

    def start(copies):
        for way, copy in copies:
            pl.when(sends[way])(copy.start)

    def arrive(copies, clear):
        for way, copy in copies:
            pl.when(arrives[way])(copy.wait_recv)
            pl.when(jnp.logical_not(arrives[way]))(functools.partial(clear, way))

    def depth_copy(step, way, k, source, target):
        side = ("up", "down").index(way)
        rows = pl.ds(BLOCK * k, BLOCK)
        return way, pltpu.make_async_remote_copy(
            src_ref=source[:, rows],
            dst_ref=target.at[:, (0, DEPTH + 1)[side], rows],
            send_sem=z_send.at[step, side, k],
            recv_sem=z_recv.at[step, side, k],
            device_id=(above, below)[side],
            device_id_type=MESH,
        )

    class Layer:
        def __init__(self, ref, z):
            self.ref, self.z = ref, z

        def __getitem__(self, at):
            return self.ref.at[at[0], self.z, at[1]]

    depth0 = {
        (way, k): depth_copy(0, way, k, Layer(fields, z), pad0)
        for k in inner + outer
        for way, z in (("up", DEPTH - 1), ("down", 0))
    }
    depth1 = {
        (way, k): depth_copy(1, way, k, Layer(pad1, z), pad1)
        for k in inner + outer
        for way, z in (("up", DEPTH), ("down", 1))
    }
    start(depth0.values())
    pass_on(0, ring_y)

    def row_copies(step, source, target):
        return [
            (
                way,
                pltpu.make_async_remote_copy(
                    src_ref=source.at[side],
                    dst_ref=target.at[side],
                    send_sem=y_send.at[step, side],
                    recv_sem=y_recv.at[step, side],
                    device_id=device,
                    device_id_type=MESH,
                ),
            )
            for side, way, device in ((0, "south", south), (1, "north", north))
        ]

    def pack_rows(source, target):
        for s in range(2):
            for z in range(DEPTH):
                target[0, s, z] = source[s, z + 1, BLOCK * groups - 1 : BLOCK * groups, :]
                target[1, s, z] = source[s, z + 1, 0:1, :]

    for k in outer:
        loads[k].wait()
    pack_rows(pad0, edge0)
    rows0 = row_copies(0, edge0, edge0_in)
    rows1 = row_copies(1, edge1, edge1_in)
    start(rows0)

    for copy in tables:
        copy.wait()
    load_classes.wait()

    def pick(bits, values):
        for bit in bits:
            values = [jnp.where(bit, high, low) for low, high in zip(values[::2], values[1::2])]
        return values[0]

    def look_up(target, values):
        splat = [[jnp.full((BLOCK, COLS), x, F32) for x in v] for v in values]

        def body(z, carry):
            for k in range(groups):
                c = cls[z, span(k), :]
                bits = [(c & bit) != 0 for bit in (1, 2, 4)]
                for s, v in enumerate(splat):
                    target[s, z, span(k), :] = pick(bits, v)
            return carry

        lax.fori_loop(0, DEPTH, body, 0)

    look_up(rates, [[diff_s[s, m] for m in range(NCLASS)] for s in range(2)])
    for k in inner:
        loads[k].wait()
    heard(0)
    pass_on(1, ring_y)

    sub = lax.broadcasted_iota(jnp.int32, (BLOCK, COLS), 0)
    col = lax.broadcasted_iota(jnp.int32, (BLOCK, COLS), 1)
    top, bottom = sub == 0, sub == BLOCK - 1
    left, right = col == 0, col == COLS - 1

    def around(source, edges, s, z, k):
        centre = source[s, z + 1, span(k), :]
        if k == 0:
            before = edges[0, s, z]
        else:
            before = source[s, z + 1, BLOCK * k - 1 : BLOCK * k, :]
        if k == groups - 1:
            after = edges[1, s, z]
        else:
            after = source[s, z + 1, BLOCK * k + BLOCK : BLOCK * k + BLOCK + 1, :]
        total = source[s, z + 2, span(k), :] + source[s, z, span(k), :]
        total = total + jnp.where(bottom, after, pltpu.roll(centre, BLOCK - 1, 0))
        total = total + jnp.where(top, before, pltpu.roll(centre, 1, 0))
        total = total + jnp.where(right, 0.0, pltpu.roll(centre, COLS - 1, 1))
        total = total + jnp.where(left, 0.0, pltpu.roll(centre, 1, 1))
        return centre, total - 6.0 * centre

    def advance(source, edges, z, k):
        u, lap_u = around(source, edges, 0, z, k)
        v, lap_v = around(source, edges, 1, z, k)
        growth = u * v * v
        new_u = u + rates[0, z, span(k), :] * lap_u - growth + FEED_RATE * (1.0 - u)
        new_v = v + rates[1, z, span(k), :] * lap_v + growth - (FEED_RATE + KILL_RATE) * v
        return new_u, new_v

    def first_update(z, k):
        new_u, new_v = advance(pad0, edge0_in, z, k)
        pad1[0, z + 1, span(k), :] = new_u
        pad1[1, z + 1, span(k), :] = new_v

    def clear_rows(target):
        def clear(way):
            for s in range(2):
                for z in range(DEPTH):
                    target[("south", "north").index(way), s, z] = jnp.zeros((1, COLS), F32)

        return clear

    def clear_depth(target, k):
        def clear(way):
            for s in range(2):
                target[s, 0 if way == "up" else DEPTH + 1, span(k), :] = jnp.zeros((BLOCK, COLS), F32)

        return clear

    def over_layers(update, blocks):
        def body(z, carry):
            for k in blocks:
                update(z, k)
            return carry

        if blocks:
            lax.fori_loop(1, DEPTH - 1, body, 0)

    over_layers(first_update, inner)
    heard(1)
    pass_on(2, ring_y)

    def outermost(k):
        for way, z, back in (("up", 0, "down"), ("down", DEPTH - 1, "up")):
            arrive([depth0[way, k]], clear_depth(pad0, k))
            first_update(z, k)
            start([depth1[back, k]])

    for k in inner:
        outermost(k)
    arrive(rows0, clear_rows(edge0_in))
    for k in outer:
        outermost(k)
    over_layers(first_update, outer)
    pack_rows(pad1, edge1)
    start(rows1)

    bins = [bin_s[m] for m in range(NCLASS)]
    scale = (1.0, 1.0, 1.0, -depth_step)
    look_up(look, [[trans_s[c, b] * scale[c] for b in bins] for c in range(4)])
    heard(2)
    pass_on(3, ring_x)

    def second_update(z, k):
        new_u, new_v = advance(pad1, edge1_in, z, k)
        final[0, z, span(k), :] = new_u
        final[1, z, span(k), :] = new_v
        passed = jnp.exp(look[3, z, span(k), :] * (0.25 + new_v * new_v))
        return new_u, passed

    for k in range(groups):
        mid[3, span(k), :] = jnp.ones((BLOCK, COLS), F32)
        for c in range(3):
            mid[c, span(k), :] = jnp.zeros((BLOCK, COLS), F32)

    def middle(z, k):
        new_u, passed = second_update(z, k)
        transmit = mid[3, span(k), :]
        weight = transmit * (1.0 - passed) * new_u
        for c in range(3):
            mid[c, span(k), :] = mid[c, span(k), :] + weight * look[c, z, span(k), :]
        mid[3, span(k), :] = transmit * passed

    over_layers(middle, inner)
    heard(3)
    pass_on(4, ring_x)
    arrive(rows1, clear_rows(edge1_in))
    over_layers(middle, outer)

    tiles = COLS // LANES // nc
    swaps = []
    for k in inner + outer:
        for way in ("up", "down"):
            arrive([depth1[way, k]], clear_depth(pad1, k))
        front_u, front_t = second_update(0, k)
        back_u, back_t = second_update(DEPTH - 1, k)
        front = (1.0 - front_t) * front_u
        transmit = mid[3, span(k), :]
        back = transmit * (1.0 - back_t) * back_u
        values = [
            front * look[c, 0, span(k), :] + front_t * (mid[c, span(k), :] + back * look[c, DEPTH - 1, span(k), :])
            for c in range(3)
        ]
        values.append(front_t * transmit * back_t)
        for half in range(nc):
            place = jnp.where(pc == half, pc, nc)
            for c in range(4):
                for t in range(tiles):
                    at = LANES * (tiles * half + t)
                    halves[place, k, pl.ds(4 * t + c, BLOCK, stride=8), :] = values[c][:, at : at + LANES]
        copy = pltpu.make_async_remote_copy(
            src_ref=halves.at[nc, k],
            dst_ref=halves.at[pc, k],
            send_sem=c_send.at[k],
            recv_sem=c_recv.at[k],
            device_id=mate,
            device_id_type=MESH,
        )
        copy.start()
        swaps.append((k, copy))

    place = lax.broadcasted_iota(jnp.int32, (8, LANES), 0)
    lower = place < 4
    is_light = (place == 3) | (place == 7)
    for k, copy in swaps:
        pltpu.make_async_remote_copy(
            src_ref=halves.at[nc, k],
            dst_ref=halves.at[1 - pc, k],
            send_sem=c_send.at[k],
            recv_sem=c_recv.at[k],
            device_id=mate,
            device_id_type=MESH,
        ).wait_recv()
        for row in range(BLOCK):
            near = halves[0, k, 8 * row : 8 * row + 8, :]
            light = jnp.where(
                lower, halves[0, k, 8 * row + 3 : 8 * row + 4, :], halves[0, k, 8 * row + 7 : 8 * row + 8, :]
            )
            merged[BLOCK * k + row] = jnp.where(is_light, 0.0, near) + light * halves[1, k, 8 * row : 8 * row + 8, :]

    heard(4)

    def hops(step):
        return min(step[0], ny - step[0]) + min(step[1], nx - step[1])

    steps = sorted([(dy, dx) for dy in range(ny) for dx in range(nx)][1:], key=hops, reverse=True)
    exchange = []
    for j, (dy, dx) in enumerate(steps):
        device = shifted(dy, dx)
        row = device[0] * nx + device[1]
        copy = pltpu.make_async_remote_copy(
            src_ref=merged.at[row],
            dst_ref=gathered.at[chip],
            send_sem=e_send.at[j],
            recv_sem=e_recv.at[chip],
            device_id=device,
            device_id_type=MESH,
        )
        copy.start()
        exchange.append(copy)
    gathered[chip] = merged[chip]
    for j, (dy, dx) in enumerate(steps):
        device = shifted(dy, dx)
        row = device[0] * nx + device[1]
        pltpu.make_async_remote_copy(
            src_ref=merged.at[row],
            dst_ref=gathered.at[row],
            send_sem=e_send.at[j],
            recv_sem=e_recv.at[row],
            device_id=device,
            device_id_type=MESH,
        ).wait_recv()
    total = transmit = None
    for i in range(ny * nx):
        light = jnp.where(lower, gathered[i, 3:4, :], gathered[i, 7:8, :])
        if i == 0:
            total, transmit = gathered[i], light
        else:
            total, transmit = total + transmit * gathered[i], transmit * light
    pixels[...] = jnp.where(is_light, 1.0 - transmit, total)

    for way, copy in list(depth0.values()) + list(depth1.values()) + rows0 + rows1:
        pl.when(sends[way])(copy.wait_send)
    for copy in [copy for _, copy in swaps] + exchange:
        copy.wait_send()


def place_outputs(final, pixels, species, image, sem):
    store = pltpu.make_async_copy(final, species, sem)
    store.start()
    image[:, 0:LANES] = pixels[0:4, :]
    image[:, LANES : 2 * LANES] = pixels[4:8, :]
    store.wait()


def build(mesh, sizes):
    ny, nx, nc, nz = sizes
    rows = ny * nx
    groups = rows // BLOCK
    block = (2, DEPTH, rows, COLS)
    padded = (2, DEPTH + 2, rows, COLS)
    edge = (2, 2, DEPTH, 1, COLS)
    vmem = pl.BlockSpec(memory_space=pltpu.VMEM)
    hbm = pl.BlockSpec(memory_space=pltpu.HBM)
    dma = pltpu.SemaphoreType.DMA

    def shards(fields, classes, diff_table, transfer, bin_table):
        depth_step = 2.0 / (DEPTH * ny * nx * nc)
        final, pixels = pl.pallas_call(
            functools.partial(kernel, sizes, depth_step),
            out_shape=(pltpu.VMEM(block, F32), pltpu.VMEM((8, LANES), F32)),
            in_specs=[hbm] * 5,
            out_specs=(vmem, vmem),
            scratch_shapes=[
                pltpu.VMEM(padded, F32),
                pltpu.VMEM(padded, F32),
                pltpu.VMEM((DEPTH, rows, COLS), jnp.int32),
                pltpu.VMEM(block, F32),
                pltpu.VMEM((4, DEPTH, rows, COLS), F32),
                pltpu.VMEM((4, rows, COLS), F32),
                pltpu.VMEM(edge, F32),
                pltpu.VMEM(edge, F32),
                pltpu.VMEM(edge, F32),
                pltpu.VMEM(edge, F32),
                pltpu.VMEM((nc + 1, groups, 8 * BLOCK, LANES), F32),
                pltpu.VMEM((rows, 8, LANES), F32),
                pltpu.VMEM((rows, 8, LANES), F32),
                pltpu.SMEM(diff_table.shape, F32),
                pltpu.SMEM(transfer.shape, F32),
                pltpu.SMEM(bin_table.shape, jnp.int32),
                dma((groups,)),
                dma((1,)),
                dma((3,)),
                dma((2, 2, groups)),
                dma((2, 2, groups)),
                dma((2, 2)),
                dma((2, 2)),
                dma((groups,)),
                dma((groups,)),
                dma((rows,)),
                dma((rows,)),
                pltpu.SemaphoreType.REGULAR((5, 2)),
            ],
            compiler_params=pltpu.CompilerParams(
                collective_id=0, has_side_effects=True, vmem_limit_bytes=20 * 2**20
            ),
            name="gray_scott",
        )(*(pltpu.with_memory_space_constraint(x, pltpu.HBM) for x in (fields, classes, diff_table, transfer, bin_table)))
        return pl.pallas_call(
            place_outputs,
            out_shape=(jax.ShapeDtypeStruct(block, F32), jax.ShapeDtypeStruct((4, 2 * LANES), F32)),
            in_specs=[vmem, vmem],
            out_specs=(hbm, vmem),
            scratch_shapes=[dma(())],
            compiler_params=pltpu.CompilerParams(vmem_limit_bytes=8 * 2**20),
            name="place_outputs",
        )(final, pixels)

    finer = Mesh(mesh.devices.reshape(sizes), NAMES)
    return jax.shard_map(
        shards,
        mesh=finer,
        in_specs=(P(None, GZ, "pz", None), P(GZ, "pz", None), P(), P(), P()),
        out_specs=(P(None, GZ, "pz", None), P(None, ("pz",) + GZ)),
        check_vma=False,
    )


def solution(mesh):
    return build(mesh, (8, 4, 2, mesh.shape["gy"]))
```

```python
import functools

import jax
import jax.numpy as jnp
from jax import lax
from jax.experimental import pallas as pl
from jax.experimental.pallas import tpu as pltpu
from jax.sharding import Mesh
from jax.sharding import PartitionSpec as P

MESH = pl.DeviceIdType.MESH
NAMES = ("py", "px", "pc", "pz")
GZ = ("py", "px", "pc")
FEED_RATE = 0.04
KILL_RATE = 0.06
NCLASS = 8
DEPTH = 8
UNROLL = 3
COLS = 512
LANES = 128
BLOCK = 8
F32 = jnp.float32


def span(k):
    return slice(BLOCK * k, BLOCK * k + BLOCK)


def kernel(
    sizes, depth_step,
    fields, classes, diff_table, transfer, bin_table,
    final, pixels,
    pad0, pad1, cls, rates, look, mid,
    edge0, edge0_in, edge1, edge1_in,
    halves, merged, gathered,
    diff_s, trans_s, bin_s,
    load_sem, class_sem, table_sem,
    z_send, z_recv, y_send, y_recv, c_send, c_recv, e_send, e_recv, relay,
):
    ny, nx, nc, nz = sizes
    py, px, pc, pz = (lax.axis_index(name) for name in NAMES)
    slabs = ny * nx * nc
    groups = (ny * nx) // BLOCK
    inner, outer = list(range(1, groups - 1)), [0, groups - 1]
    slab = (py * nx + px) * nc + pc
    chip = py * nx + px

    def slab_device(g):
        return (lax.div(g, nx * nc), lax.rem(lax.div(g, nc), nx), lax.rem(g, nc), pz)

    above = slab_device(lax.rem(slab + 1, slabs))
    below = slab_device(lax.rem(slab + slabs - 1, slabs))
    north = (py, px, pc, lax.rem(pz + nz - 1, nz))
    south = (py, px, pc, lax.rem(pz + 1, nz))
    mate = (py, px, 1 - pc, pz)
    has_above, has_below = slab < slabs - 1, slab > 0
    has_north, has_south = pz > 0, pz < nz - 1

    def shifted(dy, dx):
        return (lax.rem(py + dy, ny), lax.rem(px + dx, nx), pc, pz)

    loads = {
        k: pltpu.make_async_copy(
            fields.at[:, :, pl.ds(BLOCK * k, BLOCK)],
            pad0.at[:, pl.ds(1, DEPTH), pl.ds(BLOCK * k, BLOCK)],
            load_sem.at[k],
        )
        for k in outer + inner
    }
    for copy in loads.values():
        copy.start()
    tables = [
        pltpu.make_async_copy(src, dst, table_sem.at[i])
        for i, (src, dst) in enumerate(((diff_table, diff_s), (transfer, trans_s), (bin_table, bin_s)))
    ]
    for copy in tables:
        copy.start()
    load_classes = pltpu.make_async_copy(classes, cls, class_sem.at[0])
    load_classes.start()

    def clear_depth(layer):
        for pad in (pad0, pad1):
            for s in range(2):
                pad[s, layer] = jnp.zeros(pad.shape[2:], F32)

    def clear_rows(side):
        for edge in (edge0_in, edge1_in):
            for s in range(2):
                edge[side, s] = jnp.zeros(edge.shape[2:], F32)

    pl.when(jnp.logical_not(has_below))(functools.partial(clear_depth, 0))
    pl.when(jnp.logical_not(has_above))(functools.partial(clear_depth, DEPTH + 1))
    pl.when(jnp.logical_not(has_north))(functools.partial(clear_rows, 0))
    pl.when(jnp.logical_not(has_south))(functools.partial(clear_rows, 1))

    barrier = pltpu.get_barrier_semaphore()

    def greet(device):
        pl.semaphore_signal(barrier, inc=1, device_id=device, device_id_type=MESH)

    ring_y = (shifted(1, 0), shifted(ny - 1, 0))
    ring_x = (shifted(0, 1), shifted(0, nx - 1))
    partners = (mate,) + ring_x + ring_y
    others = ((has_above, above), (has_below, below), (has_north, north), (has_south, south))
    count = len(partners)
    for exists, device in others:
        pl.when(exists)(functools.partial(greet, device))
        count = count + jnp.where(exists, 1, 0)
    for device in partners:
        greet(device)
    pl.semaphore_wait(barrier, count)

    def pass_on(r, ring):
        for way in range(2):
            pl.semaphore_signal(relay.at[r, way], inc=1, device_id=ring[way], device_id_type=MESH)

    def heard(r):
        for way in range(2):
            pl.semaphore_wait(relay.at[r, way], 1)

    sends = {"up": has_above, "down": has_below, "south": has_south, "north": has_north}
    arrives = {"up": has_below, "down": has_above, "south": has_north, "north": has_south}

    def start(copies):
        for way, copy in copies:
            pl.when(sends[way])(copy.start)

    def arrive(copies):
        for way, copy in copies:
            pl.when(arrives[way])(copy.wait_recv)

    def depth_copy(step, way, k, source, target):
        side = ("up", "down").index(way)
        rows = pl.ds(BLOCK * k, BLOCK)
        return way, pltpu.make_async_remote_copy(
            src_ref=source[:, rows],
            dst_ref=target.at[:, (0, DEPTH + 1)[side], rows],
            send_sem=z_send.at[step, side, k],
            recv_sem=z_recv.at[step, side, k],
            device_id=(above, below)[side],
            device_id_type=MESH,
        )

    class Layer:
        def __init__(self, ref, z):
            self.ref, self.z = ref, z

        def __getitem__(self, at):
            return self.ref.at[at[0], self.z, at[1]]

    depth0 = {
        (way, k): depth_copy(0, way, k, Layer(fields, z), pad0)
        for k in inner + outer
        for way, z in (("up", DEPTH - 1), ("down", 0))
    }
    depth1 = {
        (way, k): depth_copy(1, way, k, Layer(pad1, z), pad1)
        for k in inner + outer
        for way, z in (("up", DEPTH), ("down", 1))
    }
    start(depth0.values())
    pass_on(0, ring_y)

    def row_copies(step, source, target):
        return [
            (
                way,
                pltpu.make_async_remote_copy(
                    src_ref=source.at[side],
                    dst_ref=target.at[side],
                    send_sem=y_send.at[step, side],
                    recv_sem=y_recv.at[step, side],
                    device_id=device,
                    device_id_type=MESH,
                ),
            )
            for side, way, device in ((0, "south", south), (1, "north", north))
        ]

    def pack_rows(source, target):
        for s in range(2):
            for z in range(DEPTH):
                target[0, s, z] = source[s, z + 1, BLOCK * groups - 1 : BLOCK * groups, :]
                target[1, s, z] = source[s, z + 1, 0:1, :]

    for k in outer:
        loads[k].wait()
    pack_rows(pad0, edge0)
    rows0 = row_copies(0, edge0, edge0_in)
    rows1 = row_copies(1, edge1, edge1_in)
    start(rows0)

    for copy in tables:
        copy.wait()
    load_classes.wait()

    def pick(bits, values):
        for bit in bits:
            values = [jnp.where(bit, high, low) for low, high in zip(values[::2], values[1::2])]
        return values[0]

    def look_up(target, values):
        splat = [[jnp.full((BLOCK, COLS), x, F32) for x in v] for v in values]

        def body(z, carry):
            for k in range(groups):
                c = cls[z, span(k), :]
                bits = [(c & bit) != 0 for bit in (1, 2, 4)]
                for s, v in enumerate(splat):
                    target[s, z, span(k), :] = pick(bits, v)
            return carry

        lax.fori_loop(0, DEPTH, body, 0)

    look_up(rates, [[diff_s[s, m] for m in range(NCLASS)] for s in range(2)])
    for k in inner:
        loads[k].wait()
    heard(0)
    pass_on(1, ring_y)

    sub = lax.broadcasted_iota(jnp.int32, (BLOCK, COLS), 0)
    col = lax.broadcasted_iota(jnp.int32, (BLOCK, COLS), 1)
    top, bottom = sub == 0, sub == BLOCK - 1
    left, right = col == 0, col == COLS - 1

    def around(source, edges, s, z, k):
        centre = source[s, z + 1, span(k), :]
        if k == 0:
            before = edges[0, s, z]
        else:
            before = source[s, z + 1, BLOCK * k - 1 : BLOCK * k, :]
        if k == groups - 1:
            after = edges[1, s, z]
        else:
            after = source[s, z + 1, BLOCK * k + BLOCK : BLOCK * k + BLOCK + 1, :]
        total = source[s, z + 2, span(k), :] + source[s, z, span(k), :]
        total = total + jnp.where(bottom, after, pltpu.roll(centre, BLOCK - 1, 0))
        total = total + jnp.where(top, before, pltpu.roll(centre, 1, 0))
        total = total + jnp.where(right, 0.0, pltpu.roll(centre, COLS - 1, 1))
        total = total + jnp.where(left, 0.0, pltpu.roll(centre, 1, 1))
        return centre, total - 6.0 * centre

    def advance(source, edges, z, k):
        u, lap_u = around(source, edges, 0, z, k)
        v, lap_v = around(source, edges, 1, z, k)
        growth = u * v * v
        new_u = u + rates[0, z, span(k), :] * lap_u - growth + FEED_RATE * (1.0 - u)
        new_v = v + rates[1, z, span(k), :] * lap_v + growth - (FEED_RATE + KILL_RATE) * v
        return new_u, new_v

    def first_update(z, k):
        new_u, new_v = advance(pad0, edge0_in, z, k)
        pad1[0, z + 1, span(k), :] = new_u
        pad1[1, z + 1, span(k), :] = new_v

    def over_layers(update, blocks):
        def body(i, carry):
            for j in range(UNROLL):
                for k in blocks:
                    update(1 + UNROLL * i + j, k)
            return carry

        if blocks:
            lax.fori_loop(0, (DEPTH - 2) // UNROLL, body, 0)

    over_layers(first_update, inner)
    heard(1)
    pass_on(2, ring_y)

    def outermost(k):
        for way in ("up", "down"):
            arrive([depth0[way, k]])
        for z in (0, DEPTH - 1):
            first_update(z, k)
        for way in ("down", "up"):
            start([depth1[way, k]])

    for k in inner:
        outermost(k)
    arrive(rows0)
    for k in outer:
        outermost(k)
    over_layers(first_update, outer)
    pack_rows(pad1, edge1)
    start(rows1)

    bins = [bin_s[m] for m in range(NCLASS)]
    scale = (1.0, 1.0, 1.0, -depth_step)
    look_up(look, [[trans_s[c, b] * scale[c] for b in bins] for c in range(4)])
    heard(2)
    pass_on(3, ring_x)

    def second_update(z, k):
        new_u, new_v = advance(pad1, edge1_in, z, k)
        final[0, z, span(k), :] = new_u
        final[1, z, span(k), :] = new_v
        passed = jnp.exp(look[3, z, span(k), :] * (0.25 + new_v * new_v))
        return new_u, passed

    for k in range(groups):
        mid[3, span(k), :] = jnp.ones((BLOCK, COLS), F32)
        for c in range(3):
            mid[c, span(k), :] = jnp.zeros((BLOCK, COLS), F32)

    def middle(z, k):
        new_u, passed = second_update(z, k)
        transmit = mid[3, span(k), :]
        weight = transmit * (1.0 - passed) * new_u
        for c in range(3):
            mid[c, span(k), :] = mid[c, span(k), :] + weight * look[c, z, span(k), :]
        mid[3, span(k), :] = transmit * passed

    over_layers(middle, inner)
    heard(3)
    pass_on(4, ring_x)
    arrive(rows1)
    over_layers(middle, outer)

    tiles = COLS // LANES // nc
    swaps = []
    for k in inner + outer:
        for way in ("up", "down"):
            arrive([depth1[way, k]])
        front_u, front_t = second_update(0, k)
        back_u, back_t = second_update(DEPTH - 1, k)
        front = (1.0 - front_t) * front_u
        transmit = mid[3, span(k), :]
        back = transmit * (1.0 - back_t) * back_u
        values = [
            front * look[c, 0, span(k), :] + front_t * (mid[c, span(k), :] + back * look[c, DEPTH - 1, span(k), :])
            for c in range(3)
        ]
        values.append(front_t * transmit * back_t)
        for half in range(nc):
            place = jnp.where(pc == half, pc, nc)
            for c in range(4):
                for t in range(tiles):
                    at = LANES * (tiles * half + t)
                    halves[place, k, pl.ds(4 * t + c, BLOCK, stride=8), :] = values[c][:, at : at + LANES]
        copy = pltpu.make_async_remote_copy(
            src_ref=halves.at[nc, k],
            dst_ref=halves.at[pc, k],
            send_sem=c_send.at[k],
            recv_sem=c_recv.at[k],
            device_id=mate,
            device_id_type=MESH,
        )
        copy.start()
        swaps.append((k, copy))

    place = lax.broadcasted_iota(jnp.int32, (8, LANES), 0)
    lower = place < 4
    is_light = (place == 3) | (place == 7)
    for k, copy in swaps:
        pltpu.make_async_remote_copy(
            src_ref=halves.at[nc, k],
            dst_ref=halves.at[1 - pc, k],
            send_sem=c_send.at[k],
            recv_sem=c_recv.at[k],
            device_id=mate,
            device_id_type=MESH,
        ).wait_recv()
        for row in range(BLOCK):
            near = halves[0, k, 8 * row : 8 * row + 8, :]
            light = jnp.where(
                lower, halves[0, k, 8 * row + 3 : 8 * row + 4, :], halves[0, k, 8 * row + 7 : 8 * row + 8, :]
            )
            merged[BLOCK * k + row] = jnp.where(is_light, 0.0, near) + light * halves[1, k, 8 * row : 8 * row + 8, :]

    heard(4)

    def hops(step):
        return min(step[0], ny - step[0]) + min(step[1], nx - step[1])

    steps = sorted([(dy, dx) for dy in range(ny) for dx in range(nx)][1:], key=hops, reverse=True)
    exchange = []
    for j, (dy, dx) in enumerate(steps):
        device = shifted(dy, dx)
        row = device[0] * nx + device[1]
        copy = pltpu.make_async_remote_copy(
            src_ref=merged.at[row],
            dst_ref=gathered.at[chip],
            send_sem=e_send.at[j],
            recv_sem=e_recv.at[chip],
            device_id=device,
            device_id_type=MESH,
        )
        copy.start()
        exchange.append(copy)
    gathered[chip] = merged[chip]
    for j, (dy, dx) in enumerate(steps):
        device = shifted(dy, dx)
        row = device[0] * nx + device[1]
        pltpu.make_async_remote_copy(
            src_ref=merged.at[row],
            dst_ref=gathered.at[row],
            send_sem=e_send.at[j],
            recv_sem=e_recv.at[row],
            device_id=device,
            device_id_type=MESH,
        ).wait_recv()
    runs = []
    for first in range(0, ny * nx, 4):
        total = gathered[first]
        transmit = jnp.where(lower, gathered[first, 3:4, :], gathered[first, 7:8, :])
        for i in range(first + 1, first + 4):
            light = jnp.where(lower, gathered[i, 3:4, :], gathered[i, 7:8, :])
            total, transmit = total + transmit * gathered[i], transmit * light
        runs.append((total, transmit))
    while len(runs) > 1:
        runs = [(a + s * b, s * t) for (a, s), (b, t) in zip(runs[::2], runs[1::2])]
    total, transmit = runs[0]
    pixels[...] = jnp.where(is_light, 1.0 - transmit, total)

    for way, copy in list(depth0.values()) + list(depth1.values()) + rows0 + rows1:
        pl.when(sends[way])(copy.wait_send)
    for copy in [copy for _, copy in swaps] + exchange:
        copy.wait_send()


def place_outputs(final, pixels, species, image, picture, sems):
    store = pltpu.make_async_copy(final, species, sems.at[0])
    store.start()
    picture[:, 0:LANES] = pixels[0:4, :]
    picture[:, LANES : 2 * LANES] = pixels[4:8, :]
    show = pltpu.make_async_copy(picture, image, sems.at[1])
    show.start()
    store.wait()
    show.wait()


def build(mesh, sizes):
    ny, nx, nc, nz = sizes
    rows = ny * nx
    groups = rows // BLOCK
    block = (2, DEPTH, rows, COLS)
    padded = (2, DEPTH + 2, rows, COLS)
    edge = (2, 2, DEPTH, 1, COLS)
    vmem = pl.BlockSpec(memory_space=pltpu.VMEM)
    hbm = pl.BlockSpec(memory_space=pltpu.HBM)
    dma = pltpu.SemaphoreType.DMA

    def shards(fields, classes, diff_table, transfer, bin_table):
        depth_step = 2.0 / (DEPTH * ny * nx * nc)
        final, pixels = pl.pallas_call(
            functools.partial(kernel, sizes, depth_step),
            out_shape=(pltpu.VMEM(block, F32), pltpu.VMEM((8, LANES), F32)),
            in_specs=[hbm] * 5,
            out_specs=(vmem, vmem),
            scratch_shapes=[
                pltpu.VMEM(padded, F32),
                pltpu.VMEM(padded, F32),
                pltpu.VMEM((DEPTH, rows, COLS), jnp.int32),
                pltpu.VMEM(block, F32),
                pltpu.VMEM((4, DEPTH, rows, COLS), F32),
                pltpu.VMEM((4, rows, COLS), F32),
                pltpu.VMEM(edge, F32),
                pltpu.VMEM(edge, F32),
                pltpu.VMEM(edge, F32),
                pltpu.VMEM(edge, F32),
                pltpu.VMEM((nc + 1, groups, 8 * BLOCK, LANES), F32),
                pltpu.VMEM((rows, 8, LANES), F32),
                pltpu.VMEM((rows, 8, LANES), F32),
                pltpu.SMEM(diff_table.shape, F32),
                pltpu.SMEM(transfer.shape, F32),
                pltpu.SMEM(bin_table.shape, jnp.int32),
                dma((groups,)),
                dma((1,)),
                dma((3,)),
                dma((2, 2, groups)),
                dma((2, 2, groups)),
                dma((2, 2)),
                dma((2, 2)),
                dma((groups,)),
                dma((groups,)),
                dma((rows,)),
                dma((rows,)),
                pltpu.SemaphoreType.REGULAR((5, 2)),
            ],
            compiler_params=pltpu.CompilerParams(
                collective_id=0, has_side_effects=True, vmem_limit_bytes=20 * 2**20
            ),
            name="gray_scott",
        )(*(pltpu.with_memory_space_constraint(x, pltpu.HBM) for x in (fields, classes, diff_table, transfer, bin_table)))
        return pl.pallas_call(
            place_outputs,
            out_shape=(jax.ShapeDtypeStruct(block, F32), jax.ShapeDtypeStruct((4, 2 * LANES), F32)),
            in_specs=[vmem, vmem],
            out_specs=(hbm, hbm),
            scratch_shapes=[pltpu.VMEM((4, 2 * LANES), F32), dma((2,))],
            compiler_params=pltpu.CompilerParams(vmem_limit_bytes=8 * 2**20),
            name="place_outputs",
        )(final, pixels)

    finer = Mesh(mesh.devices.reshape(sizes), NAMES)
    return jax.shard_map(
        shards,
        mesh=finer,
        in_specs=(P(None, GZ, "pz", None), P(GZ, "pz", None), P(), P(), P()),
        out_specs=(P(None, GZ, "pz", None), P(None, ("pz",) + GZ)),
        check_vma=False,
    )


def solution(mesh):
    return build(mesh, (8, 4, 2, mesh.shape["gy"]))
```

```python
import functools

import jax
import jax.numpy as jnp
from jax import lax
from jax.experimental import pallas as pl
from jax.experimental.pallas import tpu as pltpu
from jax.sharding import Mesh
from jax.sharding import PartitionSpec as P

MESH = pl.DeviceIdType.MESH
NAMES = ("py", "px", "pc", "pz")
GZ = ("py", "px", "pc")
FEED_RATE = 0.04
KILL_RATE = 0.06
NCLASS = 8
DEPTH = 8
UNROLL = 3
COLS = 512
LANES = 128
BLOCK = 8
F32 = jnp.float32


def span(k):
    return slice(BLOCK * k, BLOCK * k + BLOCK)


def kernel(
    sizes, depth_step,
    fields, classes, diff_table, transfer, bin_table,
    final, pixels,
    pad0, pad1, cls, rates, look, mid,
    edge0, edge0_in, edge1, edge1_in,
    halves, merged, gathered,
    diff_s, trans_s, bin_s,
    load_sem, class_sem, table_sem,
    z_send, z_recv, y_send, y_recv, c_send, c_recv, e_send, e_recv, relay,
):
    ny, nx, nc, nz = sizes
    py, px, pc, pz = (lax.axis_index(name) for name in NAMES)
    slabs = ny * nx * nc
    groups = (ny * nx) // BLOCK
    inner, outer = list(range(1, groups - 1)), [0, groups - 1]
    slab = (py * nx + px) * nc + pc
    chip = py * nx + px

    def slab_device(g):
        return (lax.div(g, nx * nc), lax.rem(lax.div(g, nc), nx), lax.rem(g, nc), pz)

    above = slab_device(lax.rem(slab + 1, slabs))
    below = slab_device(lax.rem(slab + slabs - 1, slabs))
    north = (py, px, pc, lax.rem(pz + nz - 1, nz))
    south = (py, px, pc, lax.rem(pz + 1, nz))
    mate = (py, px, 1 - pc, pz)
    has_above, has_below = slab < slabs - 1, slab > 0
    has_north, has_south = pz > 0, pz < nz - 1

    def shifted(dy, dx):
        return (lax.rem(py + dy, ny), lax.rem(px + dx, nx), pc, pz)

    barrier = pltpu.get_barrier_semaphore()

    def greet(device):
        pl.semaphore_signal(barrier, inc=1, device_id=device, device_id_type=MESH)

    ring_y = (shifted(1, 0), shifted(ny - 1, 0))
    ring_x = (shifted(0, 1), shifted(0, nx - 1))
    partners = (mate,) + ring_x + ring_y
    others = ((has_above, above), (has_below, below), (has_north, north), (has_south, south))
    count = len(partners)
    for exists, device in others:
        pl.when(exists)(functools.partial(greet, device))
        count = count + jnp.where(exists, 1, 0)
    for device in partners:
        greet(device)
    loads = {
        k: pltpu.make_async_copy(
            fields.at[:, :, pl.ds(BLOCK * k, BLOCK)],
            pad0.at[:, pl.ds(1, DEPTH), pl.ds(BLOCK * k, BLOCK)],
            load_sem.at[k],
        )
        for k in outer + inner
    }
    for copy in loads.values():
        copy.start()
    tables = [
        pltpu.make_async_copy(src, dst, table_sem.at[i])
        for i, (src, dst) in enumerate(((diff_table, diff_s), (transfer, trans_s), (bin_table, bin_s)))
    ]
    for copy in tables:
        copy.start()
    load_classes = pltpu.make_async_copy(classes, cls, class_sem.at[0])
    load_classes.start()

    pl.semaphore_wait(barrier, count)

    def pass_on(r, ring):
        for way in range(2):
            pl.semaphore_signal(relay.at[r, way], inc=1, device_id=ring[way], device_id_type=MESH)

    def heard(r):
        for way in range(2):
            pl.semaphore_wait(relay.at[r, way], 1)

    sends = {"up": has_above, "down": has_below, "south": has_south, "north": has_north}
    arrives = {"up": has_below, "down": has_above, "south": has_north, "north": has_south}

    def start(copies):
        for way, copy in copies:
            pl.when(sends[way])(copy.start)

    def arrive(copies):
        for way, copy in copies:
            pl.when(arrives[way])(copy.wait_recv)

    def depth_copy(step, way, k, source, target):
        side = ("up", "down").index(way)
        rows = pl.ds(BLOCK * k, BLOCK)
        return way, pltpu.make_async_remote_copy(
            src_ref=source[:, rows],
            dst_ref=target.at[:, (0, DEPTH + 1)[side], rows],
            send_sem=z_send.at[step, side, k],
            recv_sem=z_recv.at[step, side, k],
            device_id=(above, below)[side],
            device_id_type=MESH,
        )

    class Layer:
        def __init__(self, ref, z):
            self.ref, self.z = ref, z

        def __getitem__(self, at):
            return self.ref.at[at[0], self.z, at[1]]

    depth0 = {
        (way, k): depth_copy(0, way, k, Layer(fields, z), pad0)
        for k in inner + outer
        for way, z in (("up", DEPTH - 1), ("down", 0))
    }
    depth1 = {
        (way, k): depth_copy(1, way, k, Layer(pad1, z), pad1)
        for k in inner + outer
        for way, z in (("up", DEPTH), ("down", 1))
    }
    start(depth0.values())
    pass_on(0, ring_y)

    def row_copies(step, source, target):
        return [
            (
                way,
                pltpu.make_async_remote_copy(
                    src_ref=source.at[side],
                    dst_ref=target.at[side],
                    send_sem=y_send.at[step, side],
                    recv_sem=y_recv.at[step, side],
                    device_id=device,
                    device_id_type=MESH,
                ),
            )
            for side, way, device in ((0, "south", south), (1, "north", north))
        ]

    def pack_rows(source, target):
        for s in range(2):
            for z in range(DEPTH):
                target[0, s, z] = source[s, z + 1, BLOCK * groups - 1 : BLOCK * groups, :]
                target[1, s, z] = source[s, z + 1, 0:1, :]

    for k in outer:
        loads[k].wait()
    pack_rows(pad0, edge0)
    rows0 = row_copies(0, edge0, edge0_in)
    rows1 = row_copies(1, edge1, edge1_in)
    start(rows0)

    def clear_depth(layer):
        for pad in (pad0, pad1):
            for s in range(2):
                pad[s, layer] = jnp.zeros(pad.shape[2:], F32)

    def clear_rows(side):
        for edge in (edge0_in, edge1_in):
            for s in range(2):
                edge[side, s] = jnp.zeros(edge.shape[2:], F32)

    pl.when(jnp.logical_not(has_below))(functools.partial(clear_depth, 0))
    pl.when(jnp.logical_not(has_above))(functools.partial(clear_depth, DEPTH + 1))
    pl.when(jnp.logical_not(has_north))(functools.partial(clear_rows, 0))
    pl.when(jnp.logical_not(has_south))(functools.partial(clear_rows, 1))


    for copy in tables:
        copy.wait()
    load_classes.wait()

    def pick(bits, values):
        for bit in bits:
            values = [jnp.where(bit, high, low) for low, high in zip(values[::2], values[1::2])]
        return values[0]

    def look_up(target, values):
        splat = [[jnp.full((BLOCK, COLS), x, F32) for x in v] for v in values]

        def body(z, carry):
            for k in range(groups):
                c = cls[z, span(k), :]
                bits = [(c & bit) != 0 for bit in (1, 2, 4)]
                for s, v in enumerate(splat):
                    target[s, z, span(k), :] = pick(bits, v)
            return carry

        lax.fori_loop(0, DEPTH, body, 0)

    look_up(rates, [[diff_s[s, m] for m in range(NCLASS)] for s in range(2)])
    for k in inner:
        loads[k].wait()
    heard(0)
    pass_on(1, ring_y)

    sub = lax.broadcasted_iota(jnp.int32, (BLOCK, COLS), 0)
    col = lax.broadcasted_iota(jnp.int32, (BLOCK, COLS), 1)
    top, bottom = sub == 0, sub == BLOCK - 1
    left, right = col == 0, col == COLS - 1

    def around(source, edges, s, z, k):
        centre = source[s, z + 1, span(k), :]
        if k == 0:
            before = edges[0, s, z]
        else:
            before = source[s, z + 1, BLOCK * k - 1 : BLOCK * k, :]
        if k == groups - 1:
            after = edges[1, s, z]
        else:
            after = source[s, z + 1, BLOCK * k + BLOCK : BLOCK * k + BLOCK + 1, :]
        total = source[s, z + 2, span(k), :] + source[s, z, span(k), :]
        total = total + jnp.where(bottom, after, pltpu.roll(centre, BLOCK - 1, 0))
        total = total + jnp.where(top, before, pltpu.roll(centre, 1, 0))
        total = total + jnp.where(right, 0.0, pltpu.roll(centre, COLS - 1, 1))
        total = total + jnp.where(left, 0.0, pltpu.roll(centre, 1, 1))
        return centre, total - 6.0 * centre

    def advance(source, edges, z, k):
        u, lap_u = around(source, edges, 0, z, k)
        v, lap_v = around(source, edges, 1, z, k)
        growth = u * v * v
        new_u = u + rates[0, z, span(k), :] * lap_u - growth + FEED_RATE * (1.0 - u)
        new_v = v + rates[1, z, span(k), :] * lap_v + growth - (FEED_RATE + KILL_RATE) * v
        return new_u, new_v

    def first_update(z, k):
        new_u, new_v = advance(pad0, edge0_in, z, k)
        pad1[0, z + 1, span(k), :] = new_u
        pad1[1, z + 1, span(k), :] = new_v

    def over_layers(update, blocks):
        def body(i, carry):
            for j in range(UNROLL):
                for k in blocks:
                    update(1 + UNROLL * i + j, k)
            return carry

        if blocks:
            lax.fori_loop(0, (DEPTH - 2) // UNROLL, body, 0)

    over_layers(first_update, inner)
    heard(1)
    pass_on(2, ring_y)

    def outermost(k):
        for way in ("up", "down"):
            arrive([depth0[way, k]])
        for z in (0, DEPTH - 1):
            first_update(z, k)
        for way in ("down", "up"):
            start([depth1[way, k]])

    for k in inner:
        outermost(k)
    arrive(rows0)
    for k in outer:
        outermost(k)
    over_layers(first_update, outer)
    pack_rows(pad1, edge1)
    start(rows1)

    bins = [bin_s[m] for m in range(NCLASS)]
    scale = (1.0, 1.0, 1.0, -depth_step)
    look_up(look, [[trans_s[c, b] * scale[c] for b in bins] for c in range(4)])
    heard(2)
    pass_on(3, ring_x)

    def second_update(z, k):
        new_u, new_v = advance(pad1, edge1_in, z, k)
        final[0, z, span(k), :] = new_u
        final[1, z, span(k), :] = new_v
        passed = jnp.exp(look[3, z, span(k), :] * (0.25 + new_v * new_v))
        return new_u, passed

    for k in range(groups):
        mid[3, span(k), :] = jnp.ones((BLOCK, COLS), F32)
        for c in range(3):
            mid[c, span(k), :] = jnp.zeros((BLOCK, COLS), F32)

    def middle(z, k):
        new_u, passed = second_update(z, k)
        transmit = mid[3, span(k), :]
        weight = transmit * (1.0 - passed) * new_u
        for c in range(3):
            mid[c, span(k), :] = mid[c, span(k), :] + weight * look[c, z, span(k), :]
        mid[3, span(k), :] = transmit * passed

    over_layers(middle, inner)
    heard(3)
    pass_on(4, ring_x)
    arrive(rows1)
    over_layers(middle, outer)

    tiles = COLS // LANES // nc
    swaps = []
    for k in inner + outer:
        for way in ("up", "down"):
            arrive([depth1[way, k]])
        front_u, front_t = second_update(0, k)
        back_u, back_t = second_update(DEPTH - 1, k)
        front = (1.0 - front_t) * front_u
        transmit = mid[3, span(k), :]
        back = transmit * (1.0 - back_t) * back_u
        values = [
            front * look[c, 0, span(k), :] + front_t * (mid[c, span(k), :] + back * look[c, DEPTH - 1, span(k), :])
            for c in range(3)
        ]
        values.append(front_t * transmit * back_t)
        for half in range(nc):
            place = jnp.where(pc == half, pc, nc)
            for c in range(4):
                for t in range(tiles):
                    at = LANES * (tiles * half + t)
                    halves[place, k, pl.ds(4 * t + c, BLOCK, stride=8), :] = values[c][:, at : at + LANES]
        copy = pltpu.make_async_remote_copy(
            src_ref=halves.at[nc, k],
            dst_ref=halves.at[pc, k],
            send_sem=c_send.at[k],
            recv_sem=c_recv.at[k],
            device_id=mate,
            device_id_type=MESH,
        )
        copy.start()
        swaps.append((k, copy))

    place = lax.broadcasted_iota(jnp.int32, (8, LANES), 0)
    lower = place < 4
    is_light = (place == 3) | (place == 7)
    for k, copy in swaps:
        pltpu.make_async_remote_copy(
            src_ref=halves.at[nc, k],
            dst_ref=halves.at[1 - pc, k],
            send_sem=c_send.at[k],
            recv_sem=c_recv.at[k],
            device_id=mate,
            device_id_type=MESH,
        ).wait_recv()
        for row in range(BLOCK):
            near = halves[0, k, 8 * row : 8 * row + 8, :]
            light = jnp.where(
                lower, halves[0, k, 8 * row + 3 : 8 * row + 4, :], halves[0, k, 8 * row + 7 : 8 * row + 8, :]
            )
            merged[BLOCK * k + row] = jnp.where(is_light, 0.0, near) + light * halves[1, k, 8 * row : 8 * row + 8, :]

    heard(4)

    def hops(step):
        return min(step[0], ny - step[0]) + min(step[1], nx - step[1])

    steps = sorted([(dy, dx) for dy in range(ny) for dx in range(nx)][1:], key=hops, reverse=True)
    for dy, dx in steps:
        device = shifted(dy, dx)
        row = device[0] * nx + device[1]
        pltpu.make_async_remote_copy(
            src_ref=merged.at[row],
            dst_ref=gathered.at[chip],
            send_sem=e_send.at[0],
            recv_sem=e_recv.at[0],
            device_id=device,
            device_id_type=MESH,
        ).start()
    gathered[chip] = merged[chip]
    for way, copy in list(depth0.values()) + list(depth1.values()) + rows0 + rows1:
        pl.when(sends[way])(copy.wait_send)
    for _, copy in swaps:
        copy.wait_send()
    others = pl.ds(0, ny * nx - 1)
    everything = pltpu.make_async_remote_copy(
        src_ref=merged.at[others],
        dst_ref=gathered.at[others],
        send_sem=e_send.at[0],
        recv_sem=e_recv.at[0],
        device_id=mate,
        device_id_type=MESH,
    )
    everything.wait_send()
    everything.wait_recv()
    runs = []
    for first in range(0, ny * nx, 4):
        total = gathered[first]
        transmit = jnp.where(lower, gathered[first, 3:4, :], gathered[first, 7:8, :])
        for i in range(first + 1, first + 4):
            light = jnp.where(lower, gathered[i, 3:4, :], gathered[i, 7:8, :])
            total, transmit = total + transmit * gathered[i], transmit * light
        runs.append((total, transmit))
    while len(runs) > 1:
        runs = [(a + s * b, s * t) for (a, s), (b, t) in zip(runs[::2], runs[1::2])]
    total, transmit = runs[0]
    pixels[...] = jnp.where(is_light, 1.0 - transmit, total)


def place_outputs(final, pixels, species, image, picture, sems):
    store = pltpu.make_async_copy(final, species, sems.at[0])
    store.start()
    picture[:, 0:LANES] = pixels[0:4, :]
    picture[:, LANES : 2 * LANES] = pixels[4:8, :]
    show = pltpu.make_async_copy(picture, image, sems.at[1])
    show.start()
    store.wait()
    show.wait()


def build(mesh, sizes):
    ny, nx, nc, nz = sizes
    rows = ny * nx
    groups = rows // BLOCK
    block = (2, DEPTH, rows, COLS)
    padded = (2, DEPTH + 2, rows, COLS)
    edge = (2, 2, DEPTH, 1, COLS)
    vmem = pl.BlockSpec(memory_space=pltpu.VMEM)
    hbm = pl.BlockSpec(memory_space=pltpu.HBM)
    dma = pltpu.SemaphoreType.DMA

    def shards(fields, classes, diff_table, transfer, bin_table):
        depth_step = 2.0 / (DEPTH * ny * nx * nc)
        final, pixels = pl.pallas_call(
            functools.partial(kernel, sizes, depth_step),
            out_shape=(pltpu.VMEM(block, F32), pltpu.VMEM((8, LANES), F32)),
            in_specs=[hbm] * 5,
            out_specs=(vmem, vmem),
            scratch_shapes=[
                pltpu.VMEM(padded, F32),
                pltpu.VMEM(padded, F32),
                pltpu.VMEM((DEPTH, rows, COLS), jnp.int32),
                pltpu.VMEM(block, F32),
                pltpu.VMEM((4, DEPTH, rows, COLS), F32),
                pltpu.VMEM((4, rows, COLS), F32),
                pltpu.VMEM(edge, F32),
                pltpu.VMEM(edge, F32),
                pltpu.VMEM(edge, F32),
                pltpu.VMEM(edge, F32),
                pltpu.VMEM((nc + 1, groups, 8 * BLOCK, LANES), F32),
                pltpu.VMEM((rows, 8, LANES), F32),
                pltpu.VMEM((rows, 8, LANES), F32),
                pltpu.SMEM(diff_table.shape, F32),
                pltpu.SMEM(transfer.shape, F32),
                pltpu.SMEM(bin_table.shape, jnp.int32),
                dma((groups,)),
                dma((1,)),
                dma((3,)),
                dma((2, 2, groups)),
                dma((2, 2, groups)),
                dma((2, 2)),
                dma((2, 2)),
                dma((groups,)),
                dma((groups,)),
                dma((1,)),
                dma((1,)),
                pltpu.SemaphoreType.REGULAR((5, 2)),
            ],
            compiler_params=pltpu.CompilerParams(
                collective_id=0, has_side_effects=True, vmem_limit_bytes=20 * 2**20
            ),
            name="gray_scott",
        )(*(pltpu.with_memory_space_constraint(x, pltpu.HBM) for x in (fields, classes, diff_table, transfer, bin_table)))
        return pl.pallas_call(
            place_outputs,
            out_shape=(jax.ShapeDtypeStruct(block, F32), jax.ShapeDtypeStruct((4, 2 * LANES), F32)),
            in_specs=[vmem, vmem],
            out_specs=(hbm, hbm),
            scratch_shapes=[pltpu.VMEM((4, 2 * LANES), F32), dma((2,))],
            compiler_params=pltpu.CompilerParams(vmem_limit_bytes=8 * 2**20),
            name="place_outputs",
        )(final, pixels)

    finer = Mesh(mesh.devices.reshape(sizes), NAMES)
    return jax.shard_map(
        shards,
        mesh=finer,
        in_specs=(P(None, GZ, "pz", None), P(GZ, "pz", None), P(), P(), P()),
        out_specs=(P(None, GZ, "pz", None), P(None, ("pz",) + GZ)),
        check_vma=False,
    )


def solution(mesh):
    return build(mesh, (8, 4, 2, mesh.shape["gy"]))
```

```python
import functools

import jax
import jax.numpy as jnp
from jax import lax
from jax.experimental import pallas as pl
from jax.experimental.pallas import tpu as pltpu
from jax.sharding import Mesh
from jax.sharding import PartitionSpec as P

MESH = pl.DeviceIdType.MESH
NAMES = ("py", "px", "pc", "pz")
GZ = ("py", "px", "pc")
FEED_RATE = 0.04
KILL_RATE = 0.06
NCLASS = 8
DEPTH = 8
UNROLL = 3
COLS = 512
LANES = 128
BLOCK = 8
F32 = jnp.float32


def span(k):
    return slice(BLOCK * k, BLOCK * k + BLOCK)


def kernel(
    sizes, depth_step,
    fields, classes, diff_table, transfer, bin_table,
    final, pixels,
    pad0, pad1, cls, rates, look, mid,
    edge0, edge0_in, edge1, edge1_in,
    halves, merged, gathered,
    diff_s, trans_s, bin_s,
    load_sem, class_sem, table_sem,
    z_send, z_recv, y_send, y_recv, c_send, c_recv, e_send, e_recv, relay,
):
    ny, nx, nc, nz = sizes
    py, px, pc, pz = (lax.axis_index(name) for name in NAMES)
    slabs = ny * nx * nc
    groups = (ny * nx) // BLOCK
    inner, outer = list(range(1, groups - 1)), [0, groups - 1]
    slab = (py * nx + px) * nc + pc
    chip = py * nx + px

    def slab_device(g):
        return (lax.div(g, nx * nc), lax.rem(lax.div(g, nc), nx), lax.rem(g, nc), pz)

    above = slab_device(lax.rem(slab + 1, slabs))
    below = slab_device(lax.rem(slab + slabs - 1, slabs))
    north = (py, px, pc, lax.rem(pz + nz - 1, nz))
    south = (py, px, pc, lax.rem(pz + 1, nz))
    mate = (py, px, 1 - pc, pz)
    has_above, has_below = slab < slabs - 1, slab > 0
    has_north, has_south = pz > 0, pz < nz - 1

    def shifted(dy, dx):
        return (lax.rem(py + dy, ny), lax.rem(px + dx, nx), pc, pz)

    barrier = pltpu.get_barrier_semaphore()

    def greet(device):
        pl.semaphore_signal(barrier, inc=1, device_id=device, device_id_type=MESH)

    ring_y = (shifted(1, 0), shifted(ny - 1, 0))
    ring_x = (shifted(0, 1), shifted(0, nx - 1))
    partners = (mate,) + ring_x + ring_y
    others = ((has_above, above), (has_below, below), (has_north, north), (has_south, south))
    count = len(partners)
    for exists, device in others:
        pl.when(exists)(functools.partial(greet, device))
        count = count + jnp.where(exists, 1, 0)
    for device in partners:
        greet(device)
    loads = {
        k: pltpu.make_async_copy(
            fields.at[:, :, pl.ds(BLOCK * k, BLOCK)],
            pad0.at[:, pl.ds(1, DEPTH), pl.ds(BLOCK * k, BLOCK)],
            load_sem.at[k],
        )
        for k in outer + inner
    }
    for copy in loads.values():
        copy.start()
    tables = [
        pltpu.make_async_copy(src, dst, table_sem.at[i])
        for i, (src, dst) in enumerate(((diff_table, diff_s), (transfer, trans_s), (bin_table, bin_s)))
    ]
    for copy in tables:
        copy.start()
    load_classes = pltpu.make_async_copy(classes, cls, class_sem.at[0])
    load_classes.start()

    pl.semaphore_wait(barrier, count)

    def pass_on(r, ring):
        for way in range(2):
            pl.semaphore_signal(relay.at[r, way], inc=1, device_id=ring[way], device_id_type=MESH)

    def heard(r):
        for way in range(2):
            pl.semaphore_wait(relay.at[r, way], 1)

    sends = {"up": has_above, "down": has_below, "south": has_south, "north": has_north}
    arrives = {"up": has_below, "down": has_above, "south": has_north, "north": has_south}

    def start(copies):
        for way, copy in copies:
            pl.when(sends[way])(copy.start)

    def arrive(copies):
        for way, copy in copies:
            pl.when(arrives[way])(copy.wait_recv)

    def depth_copy(step, way, k, source, target):
        side = ("up", "down").index(way)
        rows = pl.ds(BLOCK * k, BLOCK)
        return way, pltpu.make_async_remote_copy(
            src_ref=source[:, rows],
            dst_ref=target.at[:, (0, DEPTH + 1)[side], rows],
            send_sem=z_send.at[step, side, k],
            recv_sem=z_recv.at[step, side, k],
            device_id=(above, below)[side],
            device_id_type=MESH,
        )

    class Layer:
        def __init__(self, ref, z):
            self.ref, self.z = ref, z

        def __getitem__(self, at):
            return self.ref.at[at[0], self.z, at[1]]

    depth0 = {
        (way, k): depth_copy(0, way, k, Layer(fields, z), pad0)
        for k in inner + outer
        for way, z in (("up", DEPTH - 1), ("down", 0))
    }
    depth1 = {
        (way, k): depth_copy(1, way, k, Layer(pad1, z), pad1)
        for k in inner + outer
        for way, z in (("up", DEPTH), ("down", 1))
    }
    start(depth0.values())
    pass_on(0, ring_y)

    def row_copies(step, source, target):
        return [
            (
                way,
                pltpu.make_async_remote_copy(
                    src_ref=source.at[side],
                    dst_ref=target.at[side],
                    send_sem=y_send.at[step, side],
                    recv_sem=y_recv.at[step, side],
                    device_id=device,
                    device_id_type=MESH,
                ),
            )
            for side, way, device in ((0, "south", south), (1, "north", north))
        ]

    def pack_rows(source, target):
        for s in range(2):
            for z in range(DEPTH):
                target[0, s, z] = source[s, z + 1, BLOCK * groups - 1 : BLOCK * groups, :]
                target[1, s, z] = source[s, z + 1, 0:1, :]

    for k in outer:
        loads[k].wait()
    pack_rows(pad0, edge0)
    rows0 = row_copies(0, edge0, edge0_in)
    rows1 = row_copies(1, edge1, edge1_in)
    start(rows0)

    def clear_depth(layer):
        for pad in (pad0, pad1):
            for s in range(2):
                pad[s, layer] = jnp.zeros(pad.shape[2:], F32)

    def clear_rows(side):
        for edge in (edge0_in, edge1_in):
            for s in range(2):
                edge[side, s] = jnp.zeros(edge.shape[2:], F32)

    pl.when(jnp.logical_not(has_below))(functools.partial(clear_depth, 0))
    pl.when(jnp.logical_not(has_above))(functools.partial(clear_depth, DEPTH + 1))
    pl.when(jnp.logical_not(has_north))(functools.partial(clear_rows, 0))
    pl.when(jnp.logical_not(has_south))(functools.partial(clear_rows, 1))


    for copy in tables:
        copy.wait()
    load_classes.wait()

    def pick(bits, values):
        for bit in bits:
            values = [jnp.where(bit, high, low) for low, high in zip(values[::2], values[1::2])]
        return values[0]

    def look_up(target, values):
        splat = [[jnp.full((BLOCK, COLS), x, F32) for x in v] for v in values]

        def body(z, carry):
            for k in range(groups):
                c = cls[z, span(k), :]
                bits = [(c & bit) != 0 for bit in (1, 2, 4)]
                for s, v in enumerate(splat):
                    target[s, z, span(k), :] = pick(bits, v)
            return carry

        lax.fori_loop(0, DEPTH, body, 0)

    look_up(rates, [[diff_s[s, m] for m in range(NCLASS)] for s in range(2)])
    for k in inner:
        loads[k].wait()
    heard(0)
    pass_on(1, ring_y)

    sub = lax.broadcasted_iota(jnp.int32, (BLOCK, COLS), 0)
    top, bottom = sub == 0, sub == BLOCK - 1
    lane = lax.broadcasted_iota(jnp.int32, (BLOCK, LANES), 1)
    left, right = lane == 0, lane == LANES - 1

    def around(source, edges, s, z, k):
        centre = source[s, z + 1, span(k), :]
        if k == 0:
            before = edges[0, s, z]
        else:
            before = source[s, z + 1, BLOCK * k - 1 : BLOCK * k, :]
        if k == groups - 1:
            after = edges[1, s, z]
        else:
            after = source[s, z + 1, BLOCK * k + BLOCK : BLOCK * k + BLOCK + 1, :]
        total = source[s, z + 2, span(k), :] + source[s, z, span(k), :]
        total = total + jnp.where(bottom, after, pltpu.roll(centre, BLOCK - 1, 0))
        total = total + jnp.where(top, before, pltpu.roll(centre, 1, 0))
        cut = [centre[:, LANES * t : LANES * t + LANES] for t in range(COLS // LANES)]
        zero = jnp.zeros((BLOCK, LANES), F32)
        after_cut, before_cut = cut[1:] + [zero], [zero] + cut[:-1]
        right_side = [pltpu.roll(jnp.where(left, b, a), LANES - 1, 1) for a, b in zip(cut, after_cut)]
        left_side = [pltpu.roll(jnp.where(right, b, a), 1, 1) for a, b in zip(cut, before_cut)]
        total = total + (jnp.concatenate(right_side, 1) + jnp.concatenate(left_side, 1))
        return centre, total - 6.0 * centre

    def advance(source, edges, z, k):
        u, lap_u = around(source, edges, 0, z, k)
        v, lap_v = around(source, edges, 1, z, k)
        growth = u * v * v
        new_u = (1.0 - FEED_RATE) * u + rates[0, z, span(k), :] * lap_u + (FEED_RATE - growth)
        new_v = (1.0 - FEED_RATE - KILL_RATE) * v + rates[1, z, span(k), :] * lap_v + growth
        return new_u, new_v

    def first_update(z, k):
        new_u, new_v = advance(pad0, edge0_in, z, k)
        pad1[0, z + 1, span(k), :] = new_u
        pad1[1, z + 1, span(k), :] = new_v

    def over_layers(update, blocks):
        def body(i, carry):
            for j in range(UNROLL):
                for k in blocks:
                    update(1 + UNROLL * i + j, k)
            return carry

        if blocks:
            lax.fori_loop(0, (DEPTH - 2) // UNROLL, body, 0)

    over_layers(first_update, inner)
    heard(1)
    pass_on(2, ring_y)

    def outermost(k):
        for way in ("up", "down"):
            arrive([depth0[way, k]])
        for z in (0, DEPTH - 1):
            first_update(z, k)
        for way in ("down", "up"):
            start([depth1[way, k]])

    for k in inner:
        outermost(k)
    arrive(rows0)
    for k in outer:
        outermost(k)
    over_layers(first_update, outer)
    pack_rows(pad1, edge1)
    start(rows1)

    bins = [bin_s[m] for m in range(NCLASS)]
    scale = (1.0, 1.0, 1.0, -depth_step)
    look_up(look, [[trans_s[c, b] * scale[c] for b in bins] for c in range(4)])
    heard(2)
    pass_on(3, ring_x)

    def second_update(z, k):
        new_u, new_v = advance(pad1, edge1_in, z, k)
        final[0, z, span(k), :] = new_u
        final[1, z, span(k), :] = new_v
        passed = jnp.exp(look[3, z, span(k), :] * (0.25 + new_v * new_v))
        return new_u, passed

    for k in range(groups):
        mid[3, span(k), :] = jnp.ones((BLOCK, COLS), F32)
        for c in range(3):
            mid[c, span(k), :] = jnp.zeros((BLOCK, COLS), F32)

    def middle(z, k):
        new_u, passed = second_update(z, k)
        transmit = mid[3, span(k), :]
        left_over = transmit * passed
        weight = (transmit - left_over) * new_u
        for c in range(3):
            mid[c, span(k), :] = mid[c, span(k), :] + weight * look[c, z, span(k), :]
        mid[3, span(k), :] = left_over

    over_layers(middle, inner)
    heard(3)
    pass_on(4, ring_x)
    arrive(rows1)
    over_layers(middle, outer)

    tiles = COLS // LANES // nc
    swaps = []
    for k in inner + outer:
        for way in ("up", "down"):
            arrive([depth1[way, k]])
        front_u, front_t = second_update(0, k)
        back_u, back_t = second_update(DEPTH - 1, k)
        front = (1.0 - front_t) * front_u
        transmit = mid[3, span(k), :]
        back = transmit * (1.0 - back_t) * back_u
        values = [
            front * look[c, 0, span(k), :] + front_t * (mid[c, span(k), :] + back * look[c, DEPTH - 1, span(k), :])
            for c in range(3)
        ]
        values.append(front_t * transmit * back_t)
        for half in range(nc):
            place = jnp.where(pc == half, pc, nc)
            for c in range(4):
                for t in range(tiles):
                    at = LANES * (tiles * half + t)
                    halves[place, k, pl.ds(4 * t + c, BLOCK, stride=8), :] = values[c][:, at : at + LANES]
        copy = pltpu.make_async_remote_copy(
            src_ref=halves.at[nc, k],
            dst_ref=halves.at[pc, k],
            send_sem=c_send.at[k],
            recv_sem=c_recv.at[k],
            device_id=mate,
            device_id_type=MESH,
        )
        copy.start()
        swaps.append((k, copy))

    place = lax.broadcasted_iota(jnp.int32, (8, LANES), 0)
    lower = place < 4
    is_light = (place == 3) | (place == 7)
    for k, copy in swaps:
        pltpu.make_async_remote_copy(
            src_ref=halves.at[nc, k],
            dst_ref=halves.at[1 - pc, k],
            send_sem=c_send.at[k],
            recv_sem=c_recv.at[k],
            device_id=mate,
            device_id_type=MESH,
        ).wait_recv()
        for row in range(BLOCK):
            near = halves[0, k, 8 * row : 8 * row + 8, :]
            light = jnp.where(
                lower, halves[0, k, 8 * row + 3 : 8 * row + 4, :], halves[0, k, 8 * row + 7 : 8 * row + 8, :]
            )
            merged[BLOCK * k + row] = jnp.where(is_light, 0.0, near) + light * halves[1, k, 8 * row : 8 * row + 8, :]

    heard(4)

    def hops(step):
        return min(step[0], ny - step[0]) + min(step[1], nx - step[1])

    steps = sorted([(dy, dx) for dy in range(ny) for dx in range(nx)][1:], key=hops, reverse=True)
    for dy, dx in steps:
        device = shifted(dy, dx)
        row = device[0] * nx + device[1]
        pltpu.make_async_remote_copy(
            src_ref=merged.at[row],
            dst_ref=gathered.at[chip],
            send_sem=e_send.at[0],
            recv_sem=e_recv.at[0],
            device_id=device,
            device_id_type=MESH,
        ).start()
    gathered[chip] = merged[chip]
    for way, copy in list(depth0.values()) + list(depth1.values()) + rows0 + rows1:
        pl.when(sends[way])(copy.wait_send)
    for _, copy in swaps:
        copy.wait_send()
    others = pl.ds(0, ny * nx - 1)
    everything = pltpu.make_async_remote_copy(
        src_ref=merged.at[others],
        dst_ref=gathered.at[others],
        send_sem=e_send.at[0],
        recv_sem=e_recv.at[0],
        device_id=mate,
        device_id_type=MESH,
    )
    everything.wait_send()
    everything.wait_recv()
    runs = []
    for first in range(0, ny * nx, 4):
        total = gathered[first]
        transmit = jnp.where(lower, gathered[first, 3:4, :], gathered[first, 7:8, :])
        for i in range(first + 1, first + 4):
            light = jnp.where(lower, gathered[i, 3:4, :], gathered[i, 7:8, :])
            total, transmit = total + transmit * gathered[i], transmit * light
        runs.append((total, transmit))
    while len(runs) > 1:
        runs = [(a + s * b, s * t) for (a, s), (b, t) in zip(runs[::2], runs[1::2])]
    total, transmit = runs[0]
    pixels[...] = jnp.where(is_light, 1.0 - transmit, total)


def place_outputs(final, pixels, species, image, picture, sems):
    store = pltpu.make_async_copy(final, species, sems.at[0])
    store.start()
    picture[:, 0:LANES] = pixels[0:4, :]
    picture[:, LANES : 2 * LANES] = pixels[4:8, :]
    show = pltpu.make_async_copy(picture, image, sems.at[1])
    show.start()
    store.wait()
    show.wait()


def build(mesh, sizes):
    ny, nx, nc, nz = sizes
    rows = ny * nx
    groups = rows // BLOCK
    block = (2, DEPTH, rows, COLS)
    padded = (2, DEPTH + 2, rows, COLS)
    edge = (2, 2, DEPTH, 1, COLS)
    vmem = pl.BlockSpec(memory_space=pltpu.VMEM)
    hbm = pl.BlockSpec(memory_space=pltpu.HBM)
    dma = pltpu.SemaphoreType.DMA

    def shards(fields, classes, diff_table, transfer, bin_table):
        depth_step = 2.0 / (DEPTH * ny * nx * nc)
        final, pixels = pl.pallas_call(
            functools.partial(kernel, sizes, depth_step),
            out_shape=(pltpu.VMEM(block, F32), pltpu.VMEM((8, LANES), F32)),
            in_specs=[hbm] * 5,
            out_specs=(vmem, vmem),
            scratch_shapes=[
                pltpu.VMEM(padded, F32),
                pltpu.VMEM(padded, F32),
                pltpu.VMEM((DEPTH, rows, COLS), jnp.int32),
                pltpu.VMEM(block, F32),
                pltpu.VMEM((4, DEPTH, rows, COLS), F32),
                pltpu.VMEM((4, rows, COLS), F32),
                pltpu.VMEM(edge, F32),
                pltpu.VMEM(edge, F32),
                pltpu.VMEM(edge, F32),
                pltpu.VMEM(edge, F32),
                pltpu.VMEM((nc + 1, groups, 8 * BLOCK, LANES), F32),
                pltpu.VMEM((rows, 8, LANES), F32),
                pltpu.VMEM((rows, 8, LANES), F32),
                pltpu.SMEM(diff_table.shape, F32),
                pltpu.SMEM(transfer.shape, F32),
                pltpu.SMEM(bin_table.shape, jnp.int32),
                dma((groups,)),
                dma((1,)),
                dma((3,)),
                dma((2, 2, groups)),
                dma((2, 2, groups)),
                dma((2, 2)),
                dma((2, 2)),
                dma((groups,)),
                dma((groups,)),
                dma((1,)),
                dma((1,)),
                pltpu.SemaphoreType.REGULAR((5, 2)),
            ],
            compiler_params=pltpu.CompilerParams(
                collective_id=0, has_side_effects=True, vmem_limit_bytes=20 * 2**20
            ),
            name="gray_scott",
        )(*(pltpu.with_memory_space_constraint(x, pltpu.HBM) for x in (fields, classes, diff_table, transfer, bin_table)))
        return pl.pallas_call(
            place_outputs,
            out_shape=(jax.ShapeDtypeStruct(block, F32), jax.ShapeDtypeStruct((4, 2 * LANES), F32)),
            in_specs=[vmem, vmem],
            out_specs=(hbm, hbm),
            scratch_shapes=[pltpu.VMEM((4, 2 * LANES), F32), dma((2,))],
            compiler_params=pltpu.CompilerParams(vmem_limit_bytes=8 * 2**20),
            name="place_outputs",
        )(final, pixels)

    finer = Mesh(mesh.devices.reshape(sizes), NAMES)
    return jax.shard_map(
        shards,
        mesh=finer,
        in_specs=(P(None, GZ, "pz", None), P(GZ, "pz", None), P(), P(), P()),
        out_specs=(P(None, GZ, "pz", None), P(None, ("pz",) + GZ)),
        check_vma=False,
    )


def solution(mesh):
    return build(mesh, (8, 4, 2, mesh.shape["gy"]))
```
